32 devices in a mesh: parts: 2 (over x), space: 16 (over z, y, core).
Axes of the slice: x: 2, y: 2, z: 4, core: 2. Of those that a mesh axis runs over, the one named last changes fastest.
Arguments:
- volume: bfloat16 [64, 16, 16, 128], P(('parts', 'space')), parts along dimension 0, may hold values from -6 to 6
- first_filter: bfloat16 [3, 3, 3, 128, 128], replicated, may hold values from -0.109375 to 0.109375
- second_filter: bfloat16 [3, 3, 3, 128, 128], replicated, may hold values from -0.109375 to 0.109375
- cotangent: bfloat16 [64, 16, 16, 128], P(('parts', 'space')), parts along dimension 0, may hold values from -0.06591797 to 0.06591797
Outputs:
- response: bfloat16 [64, 16, 16, 128], P(('parts', 'space')), parts along dimension 0
- first_grad: float32 [256, 3, 3, 3, 128], P(('parts', 'space')), parts along dimension 0
- second_grad: float32 [256, 3, 3, 3, 128], P(('parts', 'space')), parts along dimension 0
The draws below stay inside these ranges and needn't reach their ends.
There are 2 independent parts, one for each index of `parts`. The reference program is written for one: setup_inputs(seed, part) draws one part's arguments, and reference() takes and returns one part's arrays. A program takes and returns all parts, laid end to end along the dimension named above; an argument that names none is the same for every part. Nothing has to cross between parts.
All inputs are finite; a program needn't handle non-finite values.
Results may differ from the reference program's by a relative error of at most 0.0049.
Values may be sent and summed in bfloat16 or wider, within the bound.
A program may use at most 64 MiB of HBM per device.

```python
import jax
import jax.numpy as jnp
from jax import lax

C = 128
CX = 16
CY = 16
NZ = 32


def spiked(drawn, own_key, source, target, blocks, factor):
    owner, partner = [(jnp.arange(drawn.shape[axis_at]) // (drawn.shape[axis_at] // blocks)).reshape([-1 if axis == axis_at else 1 for axis in range(drawn.ndim)]) for axis_at in (source, target)]
    chosen = jax.random.permutation(own_key, blocks)[partner]
    strong = (owner == chosen) | (owner == (partner + blocks // 2) % blocks)
    return jnp.where(strong, factor * drawn, drawn)


def block_scale(key, dims, pieces, smallest, largest):
    def one(axis_at, parts):
        heights = jax.random.uniform(jax.random.fold_in(jax.random.fold_in(key, 6), axis_at), (parts,), jnp.float32, smallest / len(pieces), largest / len(pieces))
        return jnp.repeat(jnp.exp(heights), dims[axis_at] // parts).reshape((-1,) + (1,) * (len(dims) - axis_at - 1))

    loudness = one(*pieces[0])
    for cut in pieces[1:]:
        loudness = loudness * one(*cut)
    return loudness


def bell_draw(stream_key, dims, scale, reach, pieces=(), held_as=jnp.bfloat16):
    gain = block_scale(stream_key, dims, pieces, -0.22, 0.18) if pieces else 1.0
    values = jax.random.normal(stream_key, dims, jnp.float32) * scale * gain
    return jnp.minimum(jnp.maximum(values, -reach), reach).astype(held_as)


def noise_with(own_key, dims, scale, reach, split, heavy, held_as=jnp.bfloat16):
    array = scale * jax.random.normal(own_key, dims, jnp.float32)
    if split:
        array = array * block_scale(own_key, dims, split, -0.22, 0.18)
    return jnp.clip(spiked(array, jax.random.fold_in(own_key, 3), *heavy), -reach, reach).astype(held_as)


def setup_inputs(seed: int = 0, part: int = 0) -> dict:
    splits = jax.random.split(jax.random.key(seed), 5)
    own_keys = jax.random.split(jax.random.fold_in(splits[4], part), 5)
    return {
        "volume": noise_with(own_keys[0], (NZ, CX, CY, C), 1.0, 6.0, ((0, 16),), (0, 3, 16, 2.0)),
        "first_filter": bell_draw(splits[1], (3, 3, 3, C, C), (27 * C) ** -0.5, 0.109375),
        "second_filter": bell_draw(splits[2], (3, 3, 3, C, C), (27 * C) ** -0.5, 0.109375),
        "cotangent": bell_draw(own_keys[3], (NZ, CX, CY, C), (1.0 / (NZ * CX * CY) ** 0.5), 0.06591797, ((0, 16),)),
    }


def spread(field):
    return jnp.pad(field, ((0, 0), (1, 1), (1, 1), (0, 0)))


def convolve(padded, weight):
    depth = padded.shape[0] - 2
    width = padded.shape[1] - 2
    height = padded.shape[2] - 2
    inner = padded.shape[3]
    total = jnp.zeros((depth * width * height, weight.shape[4]), jnp.float32)
    for plane in range(3):
        for column in range(3):
            slab = jnp.concatenate([padded[plane:plane + depth, column:column + width, lane:lane + height, :] for lane in range(3)], axis=-1)
            total = total + jnp.dot(slab.reshape(-1, 3 * inner), weight[plane, column].reshape(3 * inner, -1), preferred_element_type=jnp.float32)
    return total.reshape(depth, width, height, -1)


def weight_term(padded, grads, start, count):
    depth, width, height, outer = grads.shape
    chosen = lax.dynamic_slice_in_dim(padded, start, count, 3)
    flat = grads.reshape(-1, outer)
    blocks = []
    for plane in range(3):
        for column in range(3):
            slab = jnp.concatenate([chosen[plane:plane + depth, column:column + width, lane:lane + height, :] for lane in range(3)], axis=-1)
            term = lax.dot_general(slab.reshape(-1, 3 * count), flat, (((0,), (0,)), ((), ())), preferred_element_type=jnp.float32)
            blocks.append(term.reshape(3, count, outer))
    stacked = jnp.stack(blocks, 0).reshape(3, 3, 3, count, outer)
    return jnp.transpose(stacked, (3, 0, 1, 2, 4))


def flipped(weight):
    return jnp.swapaxes(jnp.flip(weight, (0, 1, 2)), 3, 4)


def reference(volume, first_filter, second_filter, cotangent):
    padded_in = spread(jnp.pad(volume, ((1, 1), (0, 0), (0, 0), (0, 0))))
    hidden = convolve(padded_in, first_filter)
    activated = jax.nn.silu(hidden).astype(jnp.bfloat16)
    padded_act = spread(jnp.pad(activated, ((1, 1), (0, 0), (0, 0), (0, 0))))
    response = convolve(padded_act, second_filter).astype(jnp.bfloat16)
    padded_cot = spread(jnp.pad(cotangent, ((1, 1), (0, 0), (0, 0), (0, 0))))
    act_grad = convolve(padded_cot, flipped(second_filter))
    sigma = jax.nn.sigmoid(hidden)
    hidden_grad = (act_grad * sigma * (1.0 + hidden * (1.0 - sigma))).astype(jnp.bfloat16)
    channels = volume.shape[3]
    second_grad = weight_term(padded_act, cotangent, 0, channels)
    first_grad = weight_term(padded_in, hidden_grad, 0, channels)
    return response, first_grad, second_grad
```

```python
import functools

import jax
import jax.numpy as jnp
from jax import lax
from jax.experimental import pallas as pl
from jax.experimental.pallas import tpu as pltpu
from jax.sharding import PartitionSpec as P

F32, BF16 = jnp.float32, jnp.bfloat16


def gather_taps(x_ref, plane, value, height, reverse=False):
    rows, chans = value.shape
    wide = value.astype(F32)
    lane = lax.rem(lax.broadcasted_iota(jnp.int32, (rows, chans), 0), height)
    before = jnp.where(lane == 0, 0.0, pltpu.roll(wide, 1, 0))
    after = jnp.where(lane == height - 1, 0.0, pltpu.roll(wide, rows - 1, 0))
    edge = jnp.zeros((height, chans), BF16)
    for c, shifted in enumerate((before.astype(BF16), value, after.astype(BF16))):
        for b in range(3):
            tap = b * 3 + c
            tap = 8 - tap if reverse else tap
            cols = slice(tap * chans, (tap + 1) * chans)
            if b == 1:
                x_ref[plane, :, cols] = shifted
            elif b == 0:
                x_ref[plane, :height, cols] = edge
                x_ref[plane, height:, cols] = shifted[: rows - height]
            else:
                x_ref[plane, : rows - height, cols] = shifted[height:]
                x_ref[plane, rows - height :, cols] = edge


def kernel(
    n, depth, height,
    v_ref, w1_ref, w2_ref, c_ref,
    resp_ref, g1_ref, g2_ref,
    xv, xc, xa, w2t, halo, act, hid, agr,
    part, b1, r1, b2, r2, b3, r3,
    hs, hr, s1, q1, s2, q2, s3, q3,
):
    chans = v_ref.shape[1]
    rows = v_ref.shape[0] // depth
    groups = n // 4
    share = chans // n
    me = lax.axis_index("space")
    core = lax.rem(me, 2)
    side = lax.rem(me // 2, 2)
    zme = me // 4
    mate = me + 1 - 2 * core
    across = me + 2 - 4 * side

    barrier = pltpu.get_barrier_semaphore()

    def greet(target):
        pl.semaphore_signal(
            barrier, inc=1, device_id={"space": target}, device_id_type=pl.DeviceIdType.MESH
        )

    def peer(j):
        return lax.rem(zme + j, groups)

    greet(lax.rem(me + 1, n))
    greet(lax.rem(me + n - 1, n))
    greet(across)
    for j in range(1, groups):
        greet(peer(j) * 4 + lax.rem(me, 4))

    def remote(src, dst, send, recv, target):
        return pltpu.make_async_remote_copy(
            src_ref=src, dst_ref=dst, send_sem=send, recv_sem=recv,
            device_id={"space": target}, device_id_type=pl.DeviceIdType.MESH,
        )

    def rims(k, src):
        up = remote(
            src.at[pl.ds((depth - 1) * rows, rows)], halo.at[k, 0], hs.at[k, 0], hr.at[k, 0],
            lax.rem(me + 1, n),
        )
        down = remote(
            src.at[pl.ds(0, rows)], halo.at[k, 1], hs.at[k, 1], hr.at[k, 1],
            lax.rem(me + n - 1, n),
        )
        return up, down

    def send_rims(k, src):
        up, down = rims(k, src)

        @pl.when(me < n - 1)
        def _():
            up.start()

        @pl.when(me > 0)
        def _():
            down.start()

    def take_rims(k, src):
        up, down = rims(k, src)

        @pl.when(me > 0)
        def _():
            up.wait_recv()
            down.wait_send()

        @pl.when(me < n - 1)
        def _():
            down.wait_recv()
            up.wait_send()

    def stretch(x_ref, a):
        return x_ref[a : a + depth].reshape(depth * rows, 9 * chans)

    def own_planes(x_ref, src, reverse=False):
        for p in range(depth):
            gather_taps(x_ref, p + 1, src[p * rows : (p + 1) * rows, :], height, reverse)

    def rim_planes(x_ref, k, reverse=False):
        gather_taps(x_ref, 0, halo[k, 0], height, reverse)
        gather_taps(x_ref, depth + 1, halo[k, 1], height, reverse)

    def mul(x, w):
        return jnp.dot(x, w, preferred_element_type=F32)

    @pl.when(me == 0)
    def _():
        for k in range(3):
            halo[k, 0] = jnp.zeros((rows, chans), BF16)

    @pl.when(me == n - 1)
    def _():
        for k in range(3):
            halo[k, 1] = jnp.zeros((rows, chans), BF16)

    own_planes(xv, v_ref)

    pl.semaphore_wait(barrier, 3 + groups - 1)

    send_rims(0, v_ref)
    send_rims(1, c_ref)
    hid[...] = mul(stretch(xv, 1), w1_ref[1])
    for t in range(27):
        w2t[t // 9, (t % 9) * chans : (t % 9 + 1) * chans, :] = w2_ref[t].T
    own_planes(xc, c_ref, True)
    agr[...] = mul(stretch(xc, 1), w2t[1])

    take_rims(0, v_ref)
    rim_planes(xv, 0)
    hid[...] += mul(stretch(xv, 0), w1_ref[0])
    hid[...] += mul(stretch(xv, 2), w1_ref[2])
    h = hid[...]
    act[...] = (h * jax.nn.sigmoid(h)).astype(BF16)
    send_rims(2, act)

    take_rims(1, c_ref)
    rim_planes(xc, 1, True)
    agr[...] += mul(stretch(xc, 0), w2t[2])
    agr[...] += mul(stretch(xc, 2), w2t[0])
    h = hid[...]
    s = jax.nn.sigmoid(h)
    hgrad = (agr[...] * s * (1.0 + h * (1.0 - s))).astype(BF16)

    def weight_part(k, x_ref, grads):
        for a in range(3):
            term = lax.dot_general(
                stretch(x_ref, a), grads, (((0,), (0,)), ((), ())), preferred_element_type=F32
            )
            for t in range(9):
                part[k, :, :, a * 9 + t] = term[t * chans : (t + 1) * chans].reshape(
                    n // 2, 2, share, chans
                )

    def first_hop(k):
        return remote(b1.at[k], r1.at[k], s1.at[k], q1.at[k], mate)

    def second_hop(k):
        return remote(b2.at[k], r2.at[k], s2.at[k], q2.at[k], across)

    def last_hop(k, j):
        return remote(
            b3.at[k, peer(j)], r3.at[k, zme], s3.at[k, peer(j)], q3.at[k, zme],
            peer(j) * 4 + lax.rem(me, 4),
        )

    def last_in(k, j):
        return remote(
            b3.at[k, peer(j)], r3.at[k, peer(j)], s3.at[k, peer(j)], q3.at[k, peer(j)],
            peer(j) * 4 + lax.rem(me, 4),
        )

    def go_first(k):
        def step(i, _):
            b1[k, i] = part[k, i, 1 - core].astype(BF16)
            return 0

        lax.fori_loop(0, n // 2, step, 0)
        first_hop(k).start()

    def go_second(k):
        first_hop(k).wait()

        def step(z, _):
            i = 2 * z + 1 - side
            b2[k, z] = (part[k, i, core] + r1[k, i].astype(F32)).astype(BF16)
            return 0

        lax.fori_loop(0, groups, step, 0)
        second_hop(k).start()

    def total(k, z):
        i = 2 * z + side
        return part[k, i, core] + r1[k, i].astype(F32) + r2[k, z].astype(F32)

    def go_last(k):
        second_hop(k).wait()
        for j in range(1, groups):
            b3[k, peer(j)] = total(k, peer(j)).astype(BF16)
            last_hop(k, j).start()

    def finish(k, out):
        whole = total(k, zme)
        for j in range(1, groups):
            last_in(k, j).wait_recv()
            whole = whole + r3[k, peer(j)].astype(F32)
        out[...] = whole
        for j in range(1, groups):
            last_hop(k, j).wait_send()

    weight_part(0, xv, hgrad)
    go_first(0)

    own_planes(xa, act)
    take_rims(2, act)
    rim_planes(xa, 2)
    go_second(0)
    weight_part(1, xa, c_ref[...])
    go_first(1)
    go_last(0)
    answer = mul(stretch(xa, 0), w2_ref[0:9].reshape(9 * chans, chans))
    answer += mul(stretch(xa, 1), w2_ref[9:18].reshape(9 * chans, chans))
    answer += mul(stretch(xa, 2), w2_ref[18:27].reshape(9 * chans, chans))
    resp_ref[...] = answer.astype(BF16)
    go_second(1)
    go_last(1)
    finish(0, g1_ref)
    finish(1, g2_ref)


def per_device(n, volume, first_filter, second_filter, cotangent):
    depth, width, height, chans = volume.shape
    rows = width * height
    share = chans // n
    groups = n // 4
    dma = pltpu.SemaphoreType.DMA
    vmem = pl.BlockSpec(memory_space=pltpu.VMEM)
    block = (27, share, chans)
    response, first, second = pl.pallas_call(
        functools.partial(kernel, n, depth, height),
        out_shape=(
            jax.ShapeDtypeStruct((depth * rows, chans), BF16),
            jax.ShapeDtypeStruct(block, F32),
            jax.ShapeDtypeStruct(block, F32),
        ),
        in_specs=[vmem] * 4,
        out_specs=(vmem,) * 3,
        scratch_shapes=[
            pltpu.VMEM((depth + 2, rows, 9 * chans), BF16),
            pltpu.VMEM((depth + 2, rows, 9 * chans), BF16),
            pltpu.VMEM((depth + 2, rows, 9 * chans), BF16),
            pltpu.VMEM((3, 9 * chans, chans), BF16),
            pltpu.VMEM((3, 2, rows, chans), BF16),
            pltpu.VMEM((depth * rows, chans), BF16),
            pltpu.VMEM((depth * rows, chans), F32),
            pltpu.VMEM((depth * rows, chans), F32),
            pltpu.VMEM((2, n // 2, 2) + block, F32),
            pltpu.VMEM((2, n // 2) + block, BF16),
            pltpu.VMEM((2, n // 2) + block, BF16),
            pltpu.VMEM((2, groups) + block, BF16),
            pltpu.VMEM((2, groups) + block, BF16),
            pltpu.VMEM((2, groups) + block, BF16),
            pltpu.VMEM((2, groups) + block, BF16),
            dma((3, 2)), dma((3, 2)),
            dma((2,)), dma((2,)), dma((2,)), dma((2,)),
            dma((2, groups)), dma((2, groups)),
        ],
        compiler_params=pltpu.CompilerParams(
            collective_id=0, has_side_effects=True, vmem_limit_bytes=60 * 1024 * 1024
        ),
    )(
        volume.reshape(depth * rows, chans),
        first_filter.reshape(3, 9 * chans, chans),
        second_filter.reshape(27, chans, chans),
        cotangent.reshape(depth * rows, chans),
    )

    def laid(grad):
        return jnp.transpose(grad, (1, 0, 2)).reshape(share, 3, 3, 3, chans)

    return response.reshape(volume.shape), laid(first), laid(second)


def solution(mesh):
    n = mesh.shape["space"]
    field = P(("parts", "space"), None, None, None)
    grad = P(("parts", "space"), None, None, None, None)
    return jax.shard_map(
        functools.partial(per_device, n),
        mesh=mesh,
        in_specs=(field, P(), P(), field),
        out_specs=(field, grad, grad),
        check_vma=False,
    )
```

```python
import functools

import jax
import jax.numpy as jnp
from jax import lax
from jax.experimental import pallas as pl
from jax.experimental.pallas import tpu as pltpu
from jax.sharding import PartitionSpec as P

F32, BF16 = jnp.float32, jnp.bfloat16


def gather_taps(x_ref, plane, value, height, reverse=False):
    rows, chans = value.shape
    wide = value.astype(F32)
    lane = lax.rem(lax.broadcasted_iota(jnp.int32, (rows, chans), 0), height)
    before = jnp.where(lane == 0, 0.0, pltpu.roll(wide, 1, 0))
    after = jnp.where(lane == height - 1, 0.0, pltpu.roll(wide, rows - 1, 0))
    edge = jnp.zeros((height, chans), BF16)
    for c, shifted in enumerate((before.astype(BF16), value, after.astype(BF16))):
        for b in range(3):
            tap = b * 3 + c
            tap = 8 - tap if reverse else tap
            cols = slice(tap * chans, (tap + 1) * chans)
            if b == 1:
                x_ref[plane, :, cols] = shifted
            elif b == 0:
                x_ref[plane, :height, cols] = edge
                x_ref[plane, height:, cols] = shifted[: rows - height]
            else:
                x_ref[plane, : rows - height, cols] = shifted[height:]
                x_ref[plane, rows - height :, cols] = edge


def kernel(
    n, depth, height,
    v_hbm, w1_hbm, w2_hbm, c_hbm,
    resp_hbm, g1_hbm, g2_hbm,
    v_ref, w1_ref, w2_ref, c_ref, resp_ref, sums, ins, outs,
    xv, xc, xa, w2t, halo, act, hid, agr,
    part, b1, r1, b2, r2, b3, r3,
    hs, hr, s1, q1, s2, q2, s3, q3,
):
    chans = v_ref.shape[1]
    rows = v_ref.shape[0] // depth
    groups = n // 4
    share = chans // n
    me = lax.axis_index("space")
    core = lax.rem(me, 2)
    side = lax.rem(me // 2, 2)
    zme = me // 4
    mate = me + 1 - 2 * core
    across = me + 2 - 4 * side

    barrier = pltpu.get_barrier_semaphore()

    def greet(target):
        pl.semaphore_signal(
            barrier, inc=1, device_id={"space": target}, device_id_type=pl.DeviceIdType.MESH
        )

    def peer(j):
        return lax.rem(zme + j, groups)

    greet(lax.rem(me + 1, n))
    greet(lax.rem(me + n - 1, n))
    greet(across)
    for j in range(1, groups):
        greet(peer(j) * 4 + lax.rem(me, 4))

    def remote(src, dst, send, recv, target):
        return pltpu.make_async_remote_copy(
            src_ref=src, dst_ref=dst, send_sem=send, recv_sem=recv,
            device_id={"space": target}, device_id_type=pl.DeviceIdType.MESH,
        )

    def load(i, src, dst):
        return pltpu.make_async_copy(src, dst, ins.at[i])

    def save(i, src, dst):
        return pltpu.make_async_copy(src, dst, outs.at[i])

    loads = (
        load(0, v_hbm, v_ref),
        load(1, c_hbm, c_ref),
        load(2, w1_hbm, w1_ref),
        load(3, w2_hbm, w2_ref),
    )
    for copy in loads:
        copy.start()

    def rims(k, src):
        up = remote(
            src.at[pl.ds((depth - 1) * rows, rows)], halo.at[k, 0], hs.at[k, 0], hr.at[k, 0],
            lax.rem(me + 1, n),
        )
        down = remote(
            src.at[pl.ds(0, rows)], halo.at[k, 1], hs.at[k, 1], hr.at[k, 1],
            lax.rem(me + n - 1, n),
        )
        return up, down

    def send_rims(k, src):
        up, down = rims(k, src)

        @pl.when(me < n - 1)
        def _():
            up.start()

        @pl.when(me > 0)
        def _():
            down.start()

    def take_rims(k, src):
        up, down = rims(k, src)

        @pl.when(me > 0)
        def _():
            up.wait_recv()
            down.wait_send()

        @pl.when(me < n - 1)
        def _():
            down.wait_recv()
            up.wait_send()

    def stretch(x_ref, a):
        return x_ref[a : a + depth].reshape(depth * rows, 9 * chans)

    def own_planes(x_ref, src, reverse=False):
        for p in range(depth):
            gather_taps(x_ref, p + 1, src[p * rows : (p + 1) * rows, :], height, reverse)

    def rim_planes(x_ref, k, reverse=False):
        gather_taps(x_ref, 0, halo[k, 0], height, reverse)
        gather_taps(x_ref, depth + 1, halo[k, 1], height, reverse)

    def mul(x, w):
        return jnp.dot(x, w, preferred_element_type=F32)

    @pl.when(me == 0)
    def _():
        for k in range(3):
            halo[k, 0] = jnp.zeros((rows, chans), BF16)

    @pl.when(me == n - 1)
    def _():
        for k in range(3):
            halo[k, 1] = jnp.zeros((rows, chans), BF16)

    loads[0].wait()
    own_planes(xv, v_ref)
    loads[1].wait()

    pl.semaphore_wait(barrier, 3 + groups - 1)

    send_rims(0, v_ref)
    send_rims(1, c_ref)
    loads[2].wait()
    hid[...] = mul(stretch(xv, 1), w1_ref[1])
    loads[3].wait()
    for t in range(27):
        w2t[t // 9, (t % 9) * chans : (t % 9 + 1) * chans, :] = w2_ref[t].T
    own_planes(xc, c_ref, True)
    agr[...] = mul(stretch(xc, 1), w2t[1])

    take_rims(0, v_ref)
    rim_planes(xv, 0)
    hid[...] += mul(stretch(xv, 0), w1_ref[0])
    hid[...] += mul(stretch(xv, 2), w1_ref[2])
    h = hid[...]
    act[...] = (h * jax.nn.sigmoid(h)).astype(BF16)
    send_rims(2, act)

    take_rims(1, c_ref)
    rim_planes(xc, 1, True)
    agr[...] += mul(stretch(xc, 0), w2t[2])
    agr[...] += mul(stretch(xc, 2), w2t[0])
    h = hid[...]
    s = jax.nn.sigmoid(h)
    hgrad = (agr[...] * s * (1.0 + h * (1.0 - s))).astype(BF16)

    def weight_part(k, x_ref, grads):
        for a in range(3):
            term = lax.dot_general(
                stretch(x_ref, a), grads, (((0,), (0,)), ((), ())), preferred_element_type=F32
            )
            for t in range(9):
                part[k, :, :, a * 9 + t] = term[t * chans : (t + 1) * chans].reshape(
                    n // 2, 2, share, chans
                )

    def first_hop(k):
        return remote(b1.at[k], r1.at[k], s1.at[k], q1.at[k], mate)

    def second_hop(k):
        return remote(b2.at[k], r2.at[k], s2.at[k], q2.at[k], across)

    def last_hop(k, j):
        return remote(
            b3.at[k, peer(j)], r3.at[k, zme], s3.at[k, peer(j)], q3.at[k, zme],
            peer(j) * 4 + lax.rem(me, 4),
        )

    def last_in(k, j):
        return remote(
            b3.at[k, peer(j)], r3.at[k, peer(j)], s3.at[k, peer(j)], q3.at[k, peer(j)],
            peer(j) * 4 + lax.rem(me, 4),
        )

    def go_first(k):
        def step(i, _):
            b1[k, i] = part[k, i, 1 - core].astype(BF16)
            return 0

        lax.fori_loop(0, n // 2, step, 0)
        first_hop(k).start()

    def go_second(k):
        first_hop(k).wait()

        def step(z, _):
            i = 2 * z + 1 - side
            b2[k, z] = (part[k, i, core] + r1[k, i].astype(F32)).astype(BF16)
            return 0

        lax.fori_loop(0, groups, step, 0)
        second_hop(k).start()

    def total(k, z):
        i = 2 * z + side
        return part[k, i, core] + r1[k, i].astype(F32) + r2[k, z].astype(F32)

    def go_last(k):
        second_hop(k).wait()
        for j in range(1, groups):
            b3[k, peer(j)] = total(k, peer(j)).astype(BF16)
            last_hop(k, j).start()

    def finish(k, out):
        whole = total(k, zme)
        for j in range(1, groups):
            last_in(k, j).wait_recv()
            whole = whole + r3[k, peer(j)].astype(F32)
        out[...] = whole
        for j in range(1, groups):
            last_hop(k, j).wait_send()

    weight_part(0, xv, hgrad)
    go_first(0)

    own_planes(xa, act)
    take_rims(2, act)
    rim_planes(xa, 2)
    go_second(0)
    weight_part(1, xa, c_ref[...])
    go_first(1)
    go_second(1)
    answer = mul(stretch(xa, 0), w2_ref[0:9].reshape(9 * chans, chans))
    answer += mul(stretch(xa, 1), w2_ref[9:18].reshape(9 * chans, chans))
    answer += mul(stretch(xa, 2), w2_ref[18:27].reshape(9 * chans, chans))
    resp_ref[...] = answer.astype(BF16)
    save(2, resp_ref, resp_hbm).start()
    go_last(0)
    go_last(1)
    finish(0, sums.at[0])
    save(0, sums.at[0], g1_hbm).start()
    finish(1, sums.at[1])
    save(1, sums.at[1], g2_hbm).start()
    save(2, resp_ref, resp_hbm).wait()
    save(0, sums.at[0], g1_hbm).wait()
    save(1, sums.at[1], g2_hbm).wait()


def per_device(n, volume, first_filter, second_filter, cotangent):
    depth, width, height, chans = volume.shape
    rows = width * height
    share = chans // n
    groups = n // 4
    dma = pltpu.SemaphoreType.DMA
    hbm = pl.BlockSpec(memory_space=pl.ANY)
    block = (27, share, chans)
    response, first, second = pl.pallas_call(
        functools.partial(kernel, n, depth, height),
        out_shape=(
            jax.ShapeDtypeStruct((depth * rows, chans), BF16),
            jax.ShapeDtypeStruct(block, F32),
            jax.ShapeDtypeStruct(block, F32),
        ),
        in_specs=[hbm] * 4,
        out_specs=(hbm,) * 3,
        scratch_shapes=[
            pltpu.VMEM((depth * rows, chans), BF16),
            pltpu.VMEM((3, 9 * chans, chans), BF16),
            pltpu.VMEM((27, chans, chans), BF16),
            pltpu.VMEM((depth * rows, chans), BF16),
            pltpu.VMEM((depth * rows, chans), BF16),
            pltpu.VMEM((2,) + block, F32),
            dma((4,)), dma((3,)),
            pltpu.VMEM((depth + 2, rows, 9 * chans), BF16),
            pltpu.VMEM((depth + 2, rows, 9 * chans), BF16),
            pltpu.VMEM((depth + 2, rows, 9 * chans), BF16),
            pltpu.VMEM((3, 9 * chans, chans), BF16),
            pltpu.VMEM((3, 2, rows, chans), BF16),
            pltpu.VMEM((depth * rows, chans), BF16),
            pltpu.VMEM((depth * rows, chans), F32),
            pltpu.VMEM((depth * rows, chans), F32),
            pltpu.VMEM((2, n // 2, 2) + block, F32),
            pltpu.VMEM((2, n // 2) + block, BF16),
            pltpu.VMEM((2, n // 2) + block, BF16),
            pltpu.VMEM((2, groups) + block, BF16),
            pltpu.VMEM((2, groups) + block, BF16),
            pltpu.VMEM((2, groups) + block, BF16),
            pltpu.VMEM((2, groups) + block, BF16),
            dma((3, 2)), dma((3, 2)),
            dma((2,)), dma((2,)), dma((2,)), dma((2,)),
            dma((2, groups)), dma((2, groups)),
        ],
        compiler_params=pltpu.CompilerParams(
            collective_id=0, has_side_effects=True, vmem_limit_bytes=60 * 1024 * 1024
        ),
    )(
        volume.reshape(depth * rows, chans),
        first_filter.reshape(3, 9 * chans, chans),
        second_filter.reshape(27, chans, chans),
        cotangent.reshape(depth * rows, chans),
    )

    def laid(grad):
        return jnp.transpose(grad, (1, 0, 2)).reshape(share, 3, 3, 3, chans)

    return response.reshape(volume.shape), laid(first), laid(second)


def solution(mesh):
    n = mesh.shape["space"]
    field = P(("parts", "space"), None, None, None)
    grad = P(("parts", "space"), None, None, None, None)
    return jax.shard_map(
        functools.partial(per_device, n),
        mesh=mesh,
        in_specs=(field, P(), P(), field),
        out_specs=(field, grad, grad),
        check_vma=False,
    )
```

```python
import functools

import jax
import jax.numpy as jnp
from jax import lax
from jax.experimental import pallas as pl
from jax.experimental.pallas import tpu as pltpu
from jax.sharding import PartitionSpec as P

F32, BF16 = jnp.float32, jnp.bfloat16


def gather_taps(x_ref, plane, value, height, reverse=False):
    rows, chans = value.shape
    wide = value.astype(F32)
    lane = lax.rem(lax.broadcasted_iota(jnp.int32, (rows, chans), 0), height)
    before = jnp.where(lane == 0, 0.0, pltpu.roll(wide, 1, 0))
    after = jnp.where(lane == height - 1, 0.0, pltpu.roll(wide, rows - 1, 0))
    edge = jnp.zeros((height, chans), BF16)
    for c, shifted in enumerate((before.astype(BF16), value, after.astype(BF16))):
        for b in range(3):
            tap = b * 3 + c
            tap = 8 - tap if reverse else tap
            cols = slice(tap * chans, (tap + 1) * chans)
            if b == 1:
                x_ref[plane, :, cols] = shifted
            elif b == 0:
                x_ref[plane, :height, cols] = edge
                x_ref[plane, height:, cols] = shifted[: rows - height]
            else:
                x_ref[plane, : rows - height, cols] = shifted[height:]
                x_ref[plane, rows - height :, cols] = edge


def kernel(
    n, depth, height,
    v_hbm, w1_hbm, w2_hbm, c_hbm,
    resp_hbm, g1_hbm, g2_hbm,
    v_ref, w1_ref, w2_ref, c_ref, resp_ref, sums, ins, outs,
    xv, xc, xa, w2t, halo, act, hid, agr,
    part, b1, r1, b2, r2, b3, r3,
    hs, hr, s1, q1, s2, q2, s3, q3,
):
    chans = v_ref.shape[1]
    rows = v_ref.shape[0] // depth
    groups = n // 4
    share = chans // n
    me = lax.axis_index("space")
    core = lax.rem(me, 2)
    side = lax.rem(me // 2, 2)
    zme = me // 4
    mate = me + 1 - 2 * core
    across = me + 2 - 4 * side

    barrier = pltpu.get_barrier_semaphore()

    def greet(target):
        pl.semaphore_signal(
            barrier, inc=1, device_id={"space": target}, device_id_type=pl.DeviceIdType.MESH
        )

    def peer(j):
        return lax.rem(zme + j, groups)

    greet(lax.rem(me + 1, n))
    greet(lax.rem(me + n - 1, n))
    greet(across)
    for j in range(1, groups):
        greet(peer(j) * 4 + lax.rem(me, 4))

    def remote(src, dst, send, recv, target):
        return pltpu.make_async_remote_copy(
            src_ref=src, dst_ref=dst, send_sem=send, recv_sem=recv,
            device_id={"space": target}, device_id_type=pl.DeviceIdType.MESH,
        )

    def load(i, src, dst):
        return pltpu.make_async_copy(src, dst, ins.at[i])

    def save(i, src, dst):
        return pltpu.make_async_copy(src, dst, outs.at[i])

    loads = (
        load(0, v_hbm, v_ref),
        load(1, c_hbm, c_ref),
        load(2, w1_hbm, w1_ref),
        load(3, w2_hbm, w2_ref),
    )
    for copy in loads:
        copy.start()

    def rims(k, src):
        up = remote(
            src.at[pl.ds((depth - 1) * rows, rows)], halo.at[k, 0], hs.at[k, 0], hr.at[k, 0],
            lax.rem(me + 1, n),
        )
        down = remote(
            src.at[pl.ds(0, rows)], halo.at[k, 1], hs.at[k, 1], hr.at[k, 1],
            lax.rem(me + n - 1, n),
        )
        return up, down

    def send_rims(k, src):
        up, down = rims(k, src)

        @pl.when(me < n - 1)
        def _():
            up.start()

        @pl.when(me > 0)
        def _():
            down.start()

    def take_rims(k, src):
        up, down = rims(k, src)

        @pl.when(me > 0)
        def _():
            up.wait_recv()
            down.wait_send()

        @pl.when(me < n - 1)
        def _():
            down.wait_recv()
            up.wait_send()

    def stretch(x_ref, a):
        return x_ref[a : a + depth].reshape(depth * rows, 9 * chans)

    def own_planes(x_ref, src, reverse=False):
        for p in range(depth):
            gather_taps(x_ref, p + 1, src[p * rows : (p + 1) * rows, :], height, reverse)

    def rim_planes(x_ref, k, reverse=False):
        gather_taps(x_ref, 0, halo[k, 0], height, reverse)
        gather_taps(x_ref, depth + 1, halo[k, 1], height, reverse)

    def mul(x, w):
        return jnp.dot(x, w, preferred_element_type=F32)

    @pl.when(me == 0)
    def _():
        for k in range(3):
            halo[k, 0] = jnp.zeros((rows, chans), BF16)

    @pl.when(me == n - 1)
    def _():
        for k in range(3):
            halo[k, 1] = jnp.zeros((rows, chans), BF16)

    loads[0].wait()
    own_planes(xv, v_ref)
    loads[1].wait()

    pl.semaphore_wait(barrier, 3 + groups - 1)

    send_rims(0, v_ref)
    send_rims(1, c_ref)
    loads[2].wait()
    hid[...] = mul(stretch(xv, 1), w1_ref[1])
    loads[3].wait()
    for t in range(27):
        w2t[t // 9, (t % 9) * chans : (t % 9 + 1) * chans, :] = w2_ref[t].T
    own_planes(xc, c_ref, True)
    agr[...] = mul(stretch(xc, 1), w2t[1])

    take_rims(0, v_ref)
    rim_planes(xv, 0)
    hid[...] += mul(stretch(xv, 0), w1_ref[0])
    hid[...] += mul(stretch(xv, 2), w1_ref[2])
    h = hid[...]
    act[...] = (h * jax.nn.sigmoid(h)).astype(BF16)
    send_rims(2, act)

    take_rims(1, c_ref)
    rim_planes(xc, 1, True)
    agr[...] += mul(stretch(xc, 0), w2t[2])
    agr[...] += mul(stretch(xc, 2), w2t[0])
    h = hid[...]
    s = jax.nn.sigmoid(h)
    hgrad = (agr[...] * s * (1.0 + h * (1.0 - s))).astype(BF16)

    def weight_piece(k, x_ref, grads):
        term = lax.dot_general(
            stretch(x_ref, k % 3), grads, (((0,), (0,)), ((), ())), preferred_element_type=F32
        )
        for t in range(9):
            part[k, :, :, t] = term[t * chans : (t + 1) * chans].reshape(
                n // 2, 2, share, chans
            )
        go_first(k)

    def first_hop(k):
        return remote(b1.at[k], r1.at[k], s1.at[k], q1.at[k], mate)

    def second_hop(k):
        return remote(b2.at[k], r2.at[k], s2.at[k], q2.at[k], across)

    def last_hop(k, j):
        return remote(
            b3.at[k, peer(j)], r3.at[k, zme], s3.at[k, peer(j)], q3.at[k, zme],
            peer(j) * 4 + lax.rem(me, 4),
        )

    def last_in(k, j):
        return remote(
            b3.at[k, peer(j)], r3.at[k, peer(j)], s3.at[k, peer(j)], q3.at[k, peer(j)],
            peer(j) * 4 + lax.rem(me, 4),
        )

    def go_first(k):
        def step(i, _):
            b1[k, i] = part[k, i, 1 - core].astype(BF16)
            return 0

        lax.fori_loop(0, n // 2, step, 0)
        first_hop(k).start()

    def go_second(k):
        first_hop(k).wait()

        def step(z, _):
            i = 2 * z + 1 - side
            b2[k, z] = (part[k, i, core] + r1[k, i].astype(F32)).astype(BF16)
            return 0

        lax.fori_loop(0, groups, step, 0)
        second_hop(k).start()

    def total(k, z):
        i = 2 * z + side
        return part[k, i, core] + r1[k, i].astype(F32) + r2[k, z].astype(F32)

    def go_last(k):
        second_hop(k).wait()
        for j in range(1, groups):
            b3[k, peer(j)] = total(k, peer(j)).astype(BF16)
            last_hop(k, j).start()

    def finish(k):
        whole = total(k, zme)
        for j in range(1, groups):
            last_in(k, j).wait_recv()
            whole = whole + r3[k, peer(j)].astype(F32)
        sums[k // 3, 9 * (k % 3) : 9 * (k % 3) + 9] = whole
        for j in range(1, groups):
            last_hop(k, j).wait_send()

    weight_piece(0, xv, hgrad)
    weight_piece(1, xv, hgrad)
    go_second(0)
    weight_piece(2, xv, hgrad)
    go_second(1)
    own_planes(xa, act)
    go_second(2)
    take_rims(2, act)
    rim_planes(xa, 2)
    weight_piece(3, xa, c_ref[...])
    weight_piece(4, xa, c_ref[...])
    go_second(3)
    go_last(0)
    weight_piece(5, xa, c_ref[...])
    go_second(4)
    go_last(1)
    go_second(5)
    answer = mul(stretch(xa, 0), w2_ref[0:9].reshape(9 * chans, chans))
    answer += mul(stretch(xa, 1), w2_ref[9:18].reshape(9 * chans, chans))
    answer += mul(stretch(xa, 2), w2_ref[18:27].reshape(9 * chans, chans))
    resp_ref[...] = answer.astype(BF16)
    save(2, resp_ref, resp_hbm).start()
    for k in range(2, 6):
        go_last(k)
    for k in range(3):
        finish(k)
    save(0, sums.at[0], g1_hbm).start()
    for k in range(3, 6):
        finish(k)
    save(1, sums.at[1], g2_hbm).start()
    save(2, resp_ref, resp_hbm).wait()
    save(0, sums.at[0], g1_hbm).wait()
    save(1, sums.at[1], g2_hbm).wait()


def per_device(n, volume, first_filter, second_filter, cotangent):
    depth, width, height, chans = volume.shape
    rows = width * height
    share = chans // n
    groups = n // 4
    dma = pltpu.SemaphoreType.DMA
    hbm = pl.BlockSpec(memory_space=pl.ANY)
    block = (27, share, chans)
    piece = (9, share, chans)
    response, first, second = pl.pallas_call(
        functools.partial(kernel, n, depth, height),
        out_shape=(
            jax.ShapeDtypeStruct((depth * rows, chans), BF16),
            jax.ShapeDtypeStruct(block, F32),
            jax.ShapeDtypeStruct(block, F32),
        ),
        in_specs=[hbm] * 4,
        out_specs=(hbm,) * 3,
        scratch_shapes=[
            pltpu.VMEM((depth * rows, chans), BF16),
            pltpu.VMEM((3, 9 * chans, chans), BF16),
            pltpu.VMEM((27, chans, chans), BF16),
            pltpu.VMEM((depth * rows, chans), BF16),
            pltpu.VMEM((depth * rows, chans), BF16),
            pltpu.VMEM((2,) + block, F32),
            dma((4,)), dma((3,)),
            pltpu.VMEM((depth + 2, rows, 9 * chans), BF16),
            pltpu.VMEM((depth + 2, rows, 9 * chans), BF16),
            pltpu.VMEM((depth + 2, rows, 9 * chans), BF16),
            pltpu.VMEM((3, 9 * chans, chans), BF16),
            pltpu.VMEM((3, 2, rows, chans), BF16),
            pltpu.VMEM((depth * rows, chans), BF16),
            pltpu.VMEM((depth * rows, chans), F32),
            pltpu.VMEM((depth * rows, chans), F32),
            pltpu.VMEM((6, n // 2, 2) + piece, F32),
            pltpu.VMEM((6, n // 2) + piece, BF16),
            pltpu.VMEM((6, n // 2) + piece, BF16),
            pltpu.VMEM((6, groups) + piece, BF16),
            pltpu.VMEM((6, groups) + piece, BF16),
            pltpu.VMEM((6, groups) + piece, BF16),
            pltpu.VMEM((6, groups) + piece, BF16),
            dma((3, 2)), dma((3, 2)),
            dma((6,)), dma((6,)), dma((6,)), dma((6,)),
            dma((6, groups)), dma((6, groups)),
        ],
        compiler_params=pltpu.CompilerParams(
            collective_id=0, has_side_effects=True, vmem_limit_bytes=60 * 1024 * 1024
        ),
    )(
        volume.reshape(depth * rows, chans),
        first_filter.reshape(3, 9 * chans, chans),
        second_filter.reshape(27, chans, chans),
        cotangent.reshape(depth * rows, chans),
    )

    def laid(grad):
        return jnp.transpose(grad, (1, 0, 2)).reshape(share, 3, 3, 3, chans)

    return response.reshape(volume.shape), laid(first), laid(second)


def solution(mesh):
    n = mesh.shape["space"]
    field = P(("parts", "space"), None, None, None)
    grad = P(("parts", "space"), None, None, None, None)
    return jax.shard_map(
        functools.partial(per_device, n),
        mesh=mesh,
        in_specs=(field, P(), P(), field),
        out_specs=(field, grad, grad),
        check_vma=False,
    )
```
